32 devices in a mesh: blk: 8 (over y, x, core), head: 4 (over z).
Axes of the slice: x: 2, y: 2, z: 4, core: 2. Of those that a mesh axis runs over, the one named last changes fastest.
Arguments:
- hidden_in: float32 [2, 2048, 2048], P(None, ('blk', 'head')), may hold values from -6 to 6
- span_order: int32 [16], replicated, may hold values from 0 to 15, each once
- attn_gain: bfloat16 [1, 2048], P(None, ('blk', 'head')), may hold values from 0.099609375 to 1.8984375
- w_query: bfloat16 [1, 2048, 2048], P(None, ('blk', 'head')), may hold values from -0.125 to 0.125
- w_key: bfloat16 [1, 2048, 256], P(None, ('blk', 'head')), may hold values from -0.125 to 0.125
- w_value: bfloat16 [1, 2048, 256], P(None, ('blk', 'head')), may hold values from -0.125 to 0.125
- w_out: bfloat16 [1, 2048, 2048], P(None, ('blk', 'head')), may hold values from -1.5 to 1.5
- ffn_gain: bfloat16 [1, 2048], P(None, ('blk', 'head')), may hold values from 0.099609375 to 1.8984375
- w_gate: bfloat16 [1, 2048, 5632], P(None, 'blk', 'head'), may hold values from -0.125 to 0.125
- w_up: bfloat16 [1, 2048, 5632], P(None, 'blk', 'head'), may hold values from -0.125 to 0.125
- w_down: bfloat16 [1, 5632, 2048], P(None, 'head', 'blk'), may hold values from -0.078125 to 0.078125
- cotangent: float32 [2, 2048, 2048], P(None, ('blk', 'head')), may hold values from -6 to 6
Outputs:
- hidden_out: float32 [2, 2048, 2048], P(None, ('blk', 'head'))
- grad_in: float32 [2, 2048, 2048], P(None, ('blk', 'head'))
- grad_attn_gain: float32 [1, 2048], P(None, ('blk', 'head'))
- grad_query_w: float32 [1, 2048, 2048], P(None, ('blk', 'head'))
- grad_key_w: float32 [1, 2048, 256], P(None, ('blk', 'head'))
- grad_value_w: float32 [1, 2048, 256], P(None, ('blk', 'head'))
- grad_out_w: float32 [1, 2048, 2048], P(None, ('blk', 'head'))
- grad_ffn_gain: float32 [1, 2048], P(None, ('blk', 'head'))
- gate_weight_gradient: float32 [1, 2048, 5632], P(None, 'blk', 'head')
- grad_up_w: float32 [1, 2048, 5632], P(None, 'blk', 'head')
- grad_down_w: float32 [1, 5632, 2048], P(None, 'head', 'blk')
The draws below stay inside these ranges and needn't reach their ends.
Inputs may be any that keep to these rules, and one draw needn't show every extreme that they name: A permutation: stored span j of each sequence (stored tokens j * 128 to (j + 1) * 128 - 1) is span span_order[j] of the sequence.
All inputs are finite; a program needn't handle non-finite values.
Results may differ from the reference program's by a relative error of at most 0.02.
Values may be sent and summed in bfloat16 or wider, within the bound.
No kernel may reach another device: no remote copies, remote signals or barrier semaphores. Data moves between devices by JAX's collectives and lax.ppermute only.
A program may use at most 192 MiB of HBM per device.

```python
import math
import jax
import jax.numpy as jnp
from jax import lax

D = 2048
HEADS = 32
KV_HEADS = 4
HEAD_DIM = 64
FF = 5632
LAYERS = 1
SEQS = 2
LEN = 2048
SPAN = 128
N_BLK = 8


def level_of(own_key, dims, shards, low, high):
    def one(dim, blocks):
        heights = jax.random.uniform(jax.random.fold_in(jax.random.fold_in(own_key, 6), dim), (blocks,), jnp.float32, low / len(shards), high / len(shards))
        return jnp.repeat(jnp.exp(heights), dims[dim] // blocks).reshape((-1,) + (1,) * (len(dims) - dim - 1))

    factor_of = one(*shards[0])
    for cut in shards[1:]:
        factor_of = factor_of * one(*cut)
    return factor_of


def normal_values(rng, extent, scale, limit, split=(), kind=jnp.bfloat16):
    array = jax.random.normal(rng, extent, jnp.float32) * scale
    if len(split) > 0:
        array = level_of(rng, extent, split, -0.22, 0.18) * array
    return jnp.clip(array, min=-limit, max=limit).astype(kind)


def setup_inputs(seed: int = 0) -> dict:
    arg_keys = jax.random.split(jax.random.key(seed), 13)
    hidden_in = normal_values(arg_keys[0], (SEQS, LEN, D), 1.0, 6.0, ((1, 32),), jnp.float32)
    span_order = jax.random.permutation(arg_keys[1], 2 * N_BLK).astype(jnp.int32)
    attn_gain = jnp.clip(1.0 + 0.18 * jax.random.normal(arg_keys[2], (LAYERS, D), jnp.float32), 0.099609375, 1.8984375).astype(jnp.bfloat16)
    w_query = normal_values(arg_keys[3], (LAYERS, D, HEADS * HEAD_DIM), D ** -0.5, 0.125, ((1, 32),))
    w_key = normal_values(arg_keys[4], (LAYERS, D, KV_HEADS * HEAD_DIM), D ** -0.5, 0.125, ((1, 32),))
    w_value = normal_values(arg_keys[5], (LAYERS, D, KV_HEADS * HEAD_DIM), D ** -0.5, 0.125, ((1, 32),))
    w_out = normal_values(arg_keys[6], (LAYERS, HEADS * HEAD_DIM, D), (max(1, D * 16 // LEN)) ** -0.5, 1.5, ((1, 32),))
    ffn_gain = jnp.clip(1.0 + 0.18 * jax.random.normal(arg_keys[7], (LAYERS, D), jnp.float32), 0.099609375, 1.8984375).astype(jnp.bfloat16)
    w_gate = normal_values(arg_keys[8], (LAYERS, D, FF), D ** -0.5, 0.125, ((1, 8), (2, 4)))
    w_up = normal_values(arg_keys[9], (LAYERS, D, FF), D ** -0.5, 0.125, ((1, 8), (2, 4)))
    w_down = normal_values(arg_keys[10], (LAYERS, FF, D), FF ** -0.5, 0.078125, ((1, 4), (2, 8)))
    cotangent = normal_values(arg_keys[11], (SEQS, LEN, D), 1.0, 6.0, ((1, 32),), jnp.float32)
    return dict(hidden_in=hidden_in, span_order=span_order, attn_gain=attn_gain, w_query=w_query, w_key=w_key, w_value=w_value, w_out=w_out, ffn_gain=ffn_gain, w_gate=w_gate, w_up=w_up, w_down=w_down, cotangent=cotangent)


EPS = 1e-05
THETA = 10000.0
NEGATIVE_PADDING = -1e+30

def round_low(values):
    return lax.optimization_barrier(values.astype(jnp.bfloat16)).astype(jnp.float32)

def rope_angles(positions, half_dim):
    inverse = 1.0 / THETA ** (jnp.arange(half_dim, dtype=jnp.float32) * (2.0 / (2 * half_dim)))
    angles = positions.astype(jnp.float32)[:, None] * inverse[None, :]
    return (jnp.cos(angles), jnp.sin(angles))

def rotate_forward(values, cosine_table, sine_table):
    half_dim = values.shape[-1] // 2
    first_half = values[..., :half_dim]
    second_half = values[..., half_dim:]
    cos_part = cosine_table[:, None, :]
    sin_part = sine_table[:, None, :]
    return jnp.concatenate([first_half * cos_part - second_half * sin_part, second_half * cos_part + first_half * sin_part], axis=-1)

def rotate_backward(gradients, cosine_table, sine_table):
    half_dim = gradients.shape[-1] // 2
    first_half = gradients[..., :half_dim]
    second_half = gradients[..., half_dim:]
    cos_part = cosine_table[:, None, :]
    sin_part = sine_table[:, None, :]
    return jnp.concatenate([first_half * cos_part + second_half * sin_part, second_half * cos_part - first_half * sin_part], axis=-1)

def rms_forward(values, gain_values):
    inverse_rms = lax.rsqrt(lax.optimization_barrier(jnp.mean(values * values, axis=-1, keepdims=True)) + EPS)
    unit_values = values * inverse_rms
    return (unit_values * gain_values, unit_values, inverse_rms)

def rms_backward(grad_normed, unit_values, inverse_rms, gain_values):
    grad_unit = grad_normed * gain_values
    value_gradient_list = inverse_rms * (grad_unit - unit_values * lax.optimization_barrier(jnp.mean(grad_unit * unit_values, axis=-1, keepdims=True)))
    grad_gain = lax.optimization_barrier(jnp.sum(grad_normed * unit_values, axis=(0, 1)))
    return (value_gradient_list, grad_gain)

def attend_forward(queries, key_heads, value_heads, positions):
    group_size = HEADS // KV_HEADS
    keys_wide = jnp.repeat(key_heads, group_size, axis=1).astype(jnp.float32)
    values_wide = jnp.repeat(value_heads, group_size, axis=1).astype(jnp.float32)
    block_rows = math.gcd(LEN, 128)
    score_scale = HEAD_DIM ** (-0.5)

    def one_block(start_row):
        rows_now = lax.dynamic_slice_in_dim(queries, start_row, block_rows, 0).astype(jnp.float32)
        row_pos = lax.dynamic_slice_in_dim(positions, start_row, block_rows, 0)
        scores = jnp.einsum('qhd,khd->hqk', rows_now, keys_wide) * score_scale
        allowed = positions[None, None, :] <= row_pos[None, :, None]
        scores = jnp.where(allowed, scores, NEGATIVE_PADDING)
        row_top = lax.optimization_barrier(jnp.max(scores, axis=-1, keepdims=True))
        row_total = lax.optimization_barrier(jnp.sum(jnp.exp(scores - row_top), axis=-1, keepdims=True))
        log_total = row_top + jnp.log(row_total)
        weights = round_low(jnp.exp(scores - log_total))
        attended = jnp.einsum('hqk,khd->qhd', weights, values_wide)
        return (attended.astype(jnp.bfloat16), log_total[..., 0])
    starts = jnp.arange(LEN // block_rows, dtype=jnp.int32) * block_rows
    attended, log_totals = lax.map(one_block, starts)
    attended = attended.reshape(LEN, HEADS, HEAD_DIM)
    log_totals = jnp.transpose(log_totals, (0, 2, 1)).reshape(LEN, HEADS)
    return (attended, log_totals)

def attend_backward(queries, key_heads, value_heads, attended, grad_attended, log_totals, positions):
    group_size = HEADS // KV_HEADS
    keys_wide = jnp.repeat(key_heads, group_size, axis=1).astype(jnp.float32)
    values_wide = jnp.repeat(value_heads, group_size, axis=1).astype(jnp.float32)
    block_rows = math.gcd(LEN, 128)
    score_scale = HEAD_DIM ** (-0.5)
    row_delta = lax.optimization_barrier(jnp.sum(grad_attended.astype(jnp.float32) * attended.astype(jnp.float32), axis=-1))

    def one_block(carried, start_row):
        key_grads, value_grads = carried
        rows_now = lax.dynamic_slice_in_dim(queries, start_row, block_rows, 0).astype(jnp.float32)
        gradient_row_block = lax.dynamic_slice_in_dim(grad_attended, start_row, block_rows, 0).astype(jnp.float32)
        row_pos = lax.dynamic_slice_in_dim(positions, start_row, block_rows, 0)
        log_rows = jnp.transpose(lax.dynamic_slice_in_dim(log_totals, start_row, block_rows, 0))
        delta_rows = jnp.transpose(lax.dynamic_slice_in_dim(row_delta, start_row, block_rows, 0))
        scores = jnp.einsum('qhd,khd->hqk', rows_now, keys_wide) * score_scale
        allowed = positions[None, None, :] <= row_pos[None, :, None]
        scores = jnp.where(allowed, scores, NEGATIVE_PADDING)
        probabilities = jnp.exp(scores - log_rows[:, :, None])
        value_grads = value_grads + jnp.einsum('hqk,qhd->khd', round_low(probabilities), gradient_row_block)
        prob_grad = jnp.einsum('qhd,khd->hqk', gradient_row_block, values_wide)
        score_grad = round_low(probabilities * (prob_grad - delta_rows[:, :, None]))
        query_grad = jnp.einsum('hqk,khd->qhd', score_grad, keys_wide) * score_scale
        key_grads = key_grads + jnp.einsum('hqk,qhd->khd', score_grad, rows_now) * score_scale
        return ((key_grads, value_grads), query_grad)
    starts = jnp.arange(LEN // block_rows, dtype=jnp.int32) * block_rows
    zero_grads = jnp.zeros((LEN, HEADS, HEAD_DIM), jnp.float32)
    (key_grads, value_grads), query_grads = lax.scan(one_block, (zero_grads, zero_grads), starts)
    query_grads = query_grads.reshape(LEN, HEADS, HEAD_DIM)
    key_grads = lax.optimization_barrier(jnp.sum(key_grads.reshape(LEN, KV_HEADS, group_size, HEAD_DIM), axis=2))
    value_grads = lax.optimization_barrier(jnp.sum(value_grads.reshape(LEN, KV_HEADS, group_size, HEAD_DIM), axis=2))
    return (query_grads, key_grads, value_grads)

def reference(hidden_in, span_order, attn_gain, w_query, w_key, w_value, w_out, ffn_gain, w_gate, w_up, w_down, cotangent):
    token_index = jnp.arange(LEN, dtype=jnp.int32)
    positions = (span_order[token_index // SPAN] * SPAN + token_index % SPAN).astype(jnp.int32)
    cosine_table, sine_table = rope_angles(positions, HEAD_DIM // 2)
    row_count = SEQS * LEN
    saved = []
    current = hidden_in
    for layer_index in range(LAYERS):
        normed_one, unit_one, inverse_one = rms_forward(current, attn_gain[layer_index].astype(jnp.float32))
        flat_one = normed_one.astype(jnp.bfloat16).reshape(row_count, D)
        query = jnp.dot(flat_one, w_query[layer_index], preferred_element_type=jnp.float32).reshape(SEQS, LEN, HEADS, HEAD_DIM)
        key_proj = jnp.dot(flat_one, w_key[layer_index], preferred_element_type=jnp.float32).reshape(SEQS, LEN, KV_HEADS, HEAD_DIM)
        value_proj = jnp.dot(flat_one, w_value[layer_index], preferred_element_type=jnp.float32).reshape(SEQS, LEN, KV_HEADS, HEAD_DIM)
        query = rotate_forward(query, cosine_table, sine_table).astype(jnp.bfloat16)
        key_proj = rotate_forward(key_proj, cosine_table, sine_table).astype(jnp.bfloat16)
        value_proj = value_proj.astype(jnp.bfloat16)
        attended_list = []
        log_list = []
        for seq_index in range(SEQS):
            attended_one, log_one = attend_forward(query[seq_index], key_proj[seq_index], value_proj[seq_index], positions)
            attended_list.append(attended_one)
            log_list.append(log_one)
        attended = jnp.stack(attended_list, axis=0)
        attended_flat = attended.reshape(row_count, HEADS * HEAD_DIM)
        middle_hidden = current + jnp.dot(attended_flat, w_out[layer_index], preferred_element_type=jnp.float32).reshape(SEQS, LEN, D)
        normed_two, unit_two, inverse_two = rms_forward(middle_hidden, ffn_gain[layer_index].astype(jnp.float32))
        flat_two = normed_two.astype(jnp.bfloat16).reshape(row_count, D)
        gate_act = jnp.dot(flat_two, w_gate[layer_index], preferred_element_type=jnp.float32)
        up_act = jnp.dot(flat_two, w_up[layer_index], preferred_element_type=jnp.float32)
        activated = (jax.nn.silu(gate_act) * up_act).astype(jnp.bfloat16)
        next_hidden = middle_hidden + jnp.dot(activated, w_down[layer_index], preferred_element_type=jnp.float32).reshape(SEQS, LEN, D)
        saved.append((flat_one, unit_one, inverse_one, query, key_proj, value_proj, attended, log_list, attended_flat, unit_two, inverse_two, flat_two))
        current = next_hidden
    hidden_out = current
    upstream = cotangent
    grads_attn_gain = [None] * LAYERS
    grads_query = [None] * LAYERS
    grads_key = [None] * LAYERS
    value_weight_gradients = [None] * LAYERS
    grads_out = [None] * LAYERS
    grads_ffn_gain = [None] * LAYERS
    grads_gate = [None] * LAYERS
    grads_up = [None] * LAYERS
    grads_down = [None] * LAYERS
    for layer_index in reversed(range(LAYERS)):
        flat_one, unit_one, inverse_one, query, key_proj, value_proj, attended, log_list, attended_flat, unit_two, inverse_two, flat_two = saved[layer_index]
        gate_act = jnp.dot(flat_two, w_gate[layer_index], preferred_element_type=jnp.float32)
        up_act = jnp.dot(flat_two, w_up[layer_index], preferred_element_type=jnp.float32)
        activated = (jax.nn.silu(gate_act) * up_act).astype(jnp.bfloat16)
        grad_low = upstream.astype(jnp.bfloat16).reshape(row_count, D)
        grads_down[layer_index] = jnp.dot(activated.T, grad_low, preferred_element_type=jnp.float32)
        grad_activated = jnp.dot(grad_low, w_down[layer_index].T, preferred_element_type=jnp.float32)
        sigmoid_gate = jax.nn.sigmoid(gate_act)
        grad_gate = (grad_activated * up_act * sigmoid_gate * (1.0 + gate_act * (1.0 - sigmoid_gate))).astype(jnp.bfloat16)
        grad_upper = (grad_activated * gate_act * sigmoid_gate).astype(jnp.bfloat16)
        grads_gate[layer_index] = jnp.dot(flat_two.T, grad_gate, preferred_element_type=jnp.float32)
        grads_up[layer_index] = jnp.dot(flat_two.T, grad_upper, preferred_element_type=jnp.float32)
        grad_normed_two = (jnp.dot(grad_gate, w_gate[layer_index].T, preferred_element_type=jnp.float32) + jnp.dot(grad_upper, w_up[layer_index].T, preferred_element_type=jnp.float32)).reshape(SEQS, LEN, D)
        grad_mid_part, gain_two_grad = rms_backward(grad_normed_two, unit_two, inverse_two, ffn_gain[layer_index].astype(jnp.float32))
        grads_ffn_gain[layer_index] = gain_two_grad
        grad_middle = upstream + grad_mid_part
        grad_mid_low = grad_middle.astype(jnp.bfloat16).reshape(row_count, D)
        grads_out[layer_index] = jnp.dot(attended_flat.T, grad_mid_low, preferred_element_type=jnp.float32)
        grad_attended = jnp.dot(grad_mid_low, w_out[layer_index].T, preferred_element_type=jnp.float32).astype(jnp.bfloat16).reshape(SEQS, LEN, HEADS, HEAD_DIM)
        query_list = []
        key_list = []
        value_list = []
        for seq_index in range(SEQS):
            query_grad, key_grad, value_grad = attend_backward(query[seq_index], key_proj[seq_index], value_proj[seq_index], attended[seq_index], grad_attended[seq_index], log_list[seq_index], positions)
            query_list.append(query_grad)
            key_list.append(key_grad)
            value_list.append(value_grad)
        query_grad = rotate_backward(jnp.stack(query_list, axis=0), cosine_table, sine_table).astype(jnp.bfloat16).reshape(row_count, HEADS * HEAD_DIM)
        key_grad = rotate_backward(jnp.stack(key_list, axis=0), cosine_table, sine_table).astype(jnp.bfloat16).reshape(row_count, KV_HEADS * HEAD_DIM)
        value_grad = jnp.stack(value_list, axis=0).astype(jnp.bfloat16).reshape(row_count, KV_HEADS * HEAD_DIM)
        grads_query[layer_index] = jnp.dot(flat_one.T, query_grad, preferred_element_type=jnp.float32)
        grads_key[layer_index] = jnp.dot(flat_one.T, key_grad, preferred_element_type=jnp.float32)
        value_weight_gradients[layer_index] = jnp.dot(flat_one.T, value_grad, preferred_element_type=jnp.float32)
        grad_normed_one = jnp.dot(query_grad, w_query[layer_index].T, preferred_element_type=jnp.float32)
        grad_normed_one = grad_normed_one + jnp.dot(key_grad, w_key[layer_index].T, preferred_element_type=jnp.float32)
        grad_normed_one = grad_normed_one + jnp.dot(value_grad, w_value[layer_index].T, preferred_element_type=jnp.float32)
        grad_in_part, gain_one_grad = rms_backward(grad_normed_one.reshape(SEQS, LEN, D), unit_one, inverse_one, attn_gain[layer_index].astype(jnp.float32))
        grads_attn_gain[layer_index] = gain_one_grad
        upstream = grad_middle + grad_in_part
    return (hidden_out, upstream, jnp.stack(grads_attn_gain, axis=0), jnp.stack(grads_query, axis=0), jnp.stack(grads_key, axis=0), jnp.stack(value_weight_gradients, axis=0), jnp.stack(grads_out, axis=0), jnp.stack(grads_ffn_gain, axis=0), jnp.stack(grads_gate, axis=0), jnp.stack(grads_up, axis=0), jnp.stack(grads_down, axis=0))
```

```python
import functools

import jax
import jax.numpy as jnp
from jax import lax
from jax.experimental import pallas as pl
from jax.experimental.pallas import tpu as pltpu
from jax.sharding import Mesh
from jax.sharding import PartitionSpec as P

HEADS = 32
KV_HEADS = 4
HD = 64
BT = 64
EPS = 1e-05
THETA = 10000.0
NEG = -1e30
LOW = jnp.bfloat16
F32 = jnp.float32

def dot_nt(a, b):
    return lax.dot_general(a, b, (((1,), (1,)), ((), ())), preferred_element_type=jnp.float32)

def dot_nn(a, b):
    return lax.dot_general(a, b, (((1,), (0,)), ((), ())), preferred_element_type=jnp.float32)

def dot_tn(a, b):
    return lax.dot_general(a, b, (((0,), (0,)), ((), ())), preferred_element_type=jnp.float32)

def stack_pairs(block, pairs, scale=None):
    rows = []
    for i in range(pairs):
        part = block[:, 128 * i:128 * i + 128]
        if scale is not None:
            part = part * scale
        lane = lax.broadcasted_iota(jnp.int32, part.shape, 1)
        zero = jnp.zeros_like(part)
        rows.append(jnp.where(lane < HD, part, zero))
        rows.append(jnp.where(lane < HD, zero, part))
    return jnp.concatenate(rows, axis=0)

def sort_keys(order_ref, kv_ref, k2, vv, blocks):
    def body(p, _):
        src = kv_ref[order_ref[p]]
        lane = lax.broadcasted_iota(jnp.int32, src.shape, 1)
        other = pltpu.roll(src.astype(jnp.float32), 64, 1).astype(src.dtype)
        dst = pl.ds(pl.multiple_of(p * BT, BT), BT)
        k2[dst, :] = jnp.where(lane < HD, src, other)
        vv[dst, :] = jnp.where(lane < HD, other, src)
        return 0
    lax.fori_loop(0, blocks, body, 0)

def visible(tile, tk, rows, qp):
    key = tile * tk + lax.broadcasted_iota(jnp.int32, (tk, rows), 0)
    query = qp * BT + (lax.broadcasted_iota(jnp.int32, (tk, rows), 1) & (BT - 1))
    return key <= query

def fwd_kernel(order_ref, qpos_ref, q_ref, kv_ref, o_ref, lse_ref, k2, vv, *, pairs, blocks, tk):
    j = pl.program_id(0)
    rows = pairs * 2 * BT
    @pl.when(j == 0)
    def _():
        sort_keys(order_ref, kv_ref, k2, vv, blocks)
    q8 = stack_pairs(q_ref[...], pairs, jnp.bfloat16(HD ** -0.5))
    qp = qpos_ref[j]
    per = tk // BT
    last = qp // per

    def step(tile, carry, masked):
        m, l, acc = carry
        ds = pl.ds(pl.multiple_of(tile * tk, tk), tk)
        s = dot_nt(k2[ds, :], q8)
        if masked:
            s = jnp.where(visible(tile, tk, rows, qp), s, NEG)
        mn = jnp.maximum(m, jnp.max(s, axis=0, keepdims=True))
        p = jnp.exp(s - mn)
        al = jnp.exp(m - mn)
        l = l * al + jnp.sum(p, axis=0, keepdims=True)
        acc = acc * al + dot_tn(vv[ds, :], p.astype(jnp.bfloat16))
        return mn, l, acc

    init = (jnp.full((1, rows), NEG, jnp.float32), jnp.zeros((1, rows), jnp.float32), jnp.zeros((128, rows), jnp.float32))
    carry = lax.fori_loop(0, last, lambda t, c: step(t, c, False), init)
    m, l, acc = step(last, carry, True)
    lse_ref[...] = (m + jnp.log(l)).reshape(lse_ref.shape)
    out = jnp.transpose(acc / l)
    lane = lax.broadcasted_iota(jnp.int32, (BT, 128), 1)
    for i in range(pairs):
        even = out[2 * i * BT:(2 * i + 1) * BT]
        odd = out[(2 * i + 1) * BT:(2 * i + 2) * BT]
        o_ref[:, 128 * i:128 * i + 128] = jnp.where(lane < HD, even, odd).astype(o_ref.dtype)

def bwd_kernel(order_ref, qpos_ref, q_ref, kv_ref, o_ref, do_ref, lse_ref, dq_ref, dkv_ref, k2, vv, dk, dv, *, pairs, blocks, tk):
    j = pl.program_id(0)
    rows = pairs * 2 * BT
    @pl.when(j == 0)
    def _():
        sort_keys(order_ref, kv_ref, k2, vv, blocks)
        dk[...] = jnp.zeros_like(dk)
        dv[...] = jnp.zeros_like(dv)
    q8 = stack_pairs(q_ref[...], pairs, jnp.bfloat16(HD ** -0.5))
    do8 = stack_pairs(do_ref[...], pairs)
    o8 = stack_pairs(o_ref[...], pairs)
    delta = jnp.sum(do8.astype(jnp.float32) * o8.astype(jnp.float32), axis=1, keepdims=True)
    delta = jnp.transpose(jnp.broadcast_to(delta, (rows, 128)))[:1]
    lse = lse_ref[...].reshape(1, rows)
    qp = qpos_ref[j]
    per = tk // BT
    last = qp // per

    def step(tile, dq, masked):
        ds = pl.ds(pl.multiple_of(tile * tk, tk), tk)
        kt = k2[ds, :]
        s = dot_nt(kt, q8)
        p = jnp.exp(s - lse)
        if masked:
            p = jnp.where(visible(tile, tk, rows, qp), p, 0.0)
        dv[ds, :] += dot_nn(p.astype(jnp.bfloat16), do8)
        dp = dot_nt(vv[ds, :], do8)
        dsc = (p * (dp - delta)).astype(jnp.bfloat16)
        dk[ds, :] += dot_nn(dsc, q8)
        return dq + dot_tn(dsc, kt)

    dq = lax.fori_loop(0, last, lambda t, c: step(t, c, False), jnp.zeros((rows, 128), jnp.float32))
    dq = step(last, dq, True) * (HD ** -0.5)
    lane = lax.broadcasted_iota(jnp.int32, (BT, 128), 1)
    for i in range(pairs):
        even = dq[2 * i * BT:(2 * i + 1) * BT]
        odd = dq[(2 * i + 1) * BT:(2 * i + 2) * BT]
        dq_ref[:, 128 * i:128 * i + 128] = jnp.where(lane < HD, even, odd)

    @pl.when(j == pl.num_programs(0) - 1)
    def _():
        def body(p, _):
            src = pl.ds(pl.multiple_of(p * BT, BT), BT)
            a = dk[src, :]
            b = dv[src, :]
            lane = lax.broadcasted_iota(jnp.int32, a.shape, 1)
            ka = a + pltpu.roll(a, 64, 1)
            vb = b + pltpu.roll(b, 64, 1)
            dkv_ref[order_ref[p]] = jnp.where(lane < HD, ka, vb).astype(dkv_ref.dtype)
            return 0
        lax.fori_loop(0, blocks, body, 0)

def attn_fwd(order, qpos, q, kv, tk=512):
    nq, width = qpos.shape[0], q.shape[1]
    pairs, blocks = width // 128, order.shape[0]
    rows = pairs * 128
    whole = lambda *s: pl.BlockSpec(s, lambda j, *_: (0,) * len(s))
    return pl.pallas_call(
        functools.partial(fwd_kernel, pairs=pairs, blocks=blocks, tk=tk),
        out_shape=(jax.ShapeDtypeStruct(q.shape, jnp.bfloat16), jax.ShapeDtypeStruct((nq, 1, rows), jnp.float32)),
        grid_spec=pltpu.PrefetchScalarGridSpec(
            num_scalar_prefetch=2, grid=(nq,),
            in_specs=[pl.BlockSpec((BT, width), lambda j, *_: (j, 0)), whole(blocks, BT, 128)],
            out_specs=[pl.BlockSpec((BT, width), lambda j, *_: (j, 0)), pl.BlockSpec((1, 1, rows), lambda j, *_: (j, 0, 0))],
            scratch_shapes=[pltpu.VMEM((blocks * BT, 128), jnp.bfloat16)] * 2),
        cost_estimate=pl.CostEstimate(flops=20_000_000_000, bytes_accessed=4 << 20, transcendentals=0),
        name="attn_fwd",
    )(order, qpos, q, kv)

def attn_bwd(order, qpos, q, kv, o, do, lse, tk=512):
    nq, width = qpos.shape[0], q.shape[1]
    pairs, blocks = width // 128, order.shape[0]
    rows = pairs * 128
    whole = lambda *s: pl.BlockSpec(s, lambda j, *_: (0,) * len(s))
    blk = pl.BlockSpec((BT, width), lambda j, *_: (j, 0))
    return pl.pallas_call(
        functools.partial(bwd_kernel, pairs=pairs, blocks=blocks, tk=tk),
        out_shape=(jax.ShapeDtypeStruct(q.shape, jnp.float32), jax.ShapeDtypeStruct((blocks, BT, 128), jnp.bfloat16)),
        grid_spec=pltpu.PrefetchScalarGridSpec(
            num_scalar_prefetch=2, grid=(nq,),
            in_specs=[blk, whole(blocks, BT, 128), blk, blk, pl.BlockSpec((1, 1, rows), lambda j, *_: (j, 0, 0))],
            out_specs=[blk, whole(blocks, BT, 128)],
            scratch_shapes=[pltpu.VMEM((blocks * BT, 128), jnp.bfloat16)] * 2 + [pltpu.VMEM((blocks * BT, 128), jnp.float32)] * 2),
        cost_estimate=pl.CostEstimate(flops=40_000_000_000, bytes_accessed=8 << 20, transcendentals=0),
        name="attn_bwd",
    )(order, qpos, q, kv, o, do, lse)


def turn(x, cos, sin):
    lane = lax.broadcasted_iota(jnp.int32, x.shape, 1) % HD
    partner = jnp.where(lane < HD // 2, pltpu.roll(x, 128 - HD // 2, 1), pltpu.roll(x, HD // 2, 1))
    return x * cos + partner * sin


def rope_kernel(x_ref, cos_ref, sin_ref, q_ref, kv_ref):
    cos, sin = cos_ref[...], sin_ref[...]
    width = q_ref.shape[1]
    for i in range(width // 128):
        part = slice(128 * i, 128 * i + 128)
        q_ref[:, part] = turn(x_ref[:, part], cos, sin).astype(LOW)
    kv = x_ref[:, width:]
    lane = lax.broadcasted_iota(jnp.int32, kv.shape, 1)
    kv_ref[...] = jnp.where(lane < HD, turn(kv, cos, sin), kv).astype(LOW)


def unrope_kernel(dq_ref, dkv_ref, cos_ref, sin_ref, d_ref):
    cos, sin = cos_ref[...], -sin_ref[...]
    width = dq_ref.shape[1]
    for i in range(width // 128):
        part = slice(128 * i, 128 * i + 128)
        d_ref[:, part] = turn(dq_ref[:, part], cos, sin).astype(LOW)
    kv = dkv_ref[...]
    lane = lax.broadcasted_iota(jnp.int32, kv.shape, 1)
    d_ref[:, width:] = jnp.where(lane < HD, turn(kv, cos, sin), kv).astype(LOW)


def rope(x, cos, sin):
    rows, width = x.shape
    tile = lambda w: pl.BlockSpec((128, w), lambda i: (i, 0))
    return pl.pallas_call(
        rope_kernel,
        grid=(rows // 128,),
        in_specs=[tile(width), tile(128), tile(128)],
        out_specs=[tile(width - 128), tile(128)],
        out_shape=(jax.ShapeDtypeStruct((rows, width - 128), LOW), jax.ShapeDtypeStruct((rows, 128), LOW)),
        cost_estimate=pl.CostEstimate(flops=8 * rows * width, bytes_accessed=6 * rows * width, transcendentals=0),
        name="rope",
    )(x, cos, sin)


def unrope(dq, dkv, cos, sin):
    rows, width = dq.shape
    tile = lambda w: pl.BlockSpec((128, w), lambda i: (i, 0))
    return pl.pallas_call(
        unrope_kernel,
        grid=(rows // 128,),
        in_specs=[tile(width), tile(128), tile(128), tile(128)],
        out_specs=tile(width + 128),
        out_shape=jax.ShapeDtypeStruct((rows, width + 128), LOW),
        cost_estimate=pl.CostEstimate(flops=8 * rows * width, bytes_accessed=6 * rows * width, transcendentals=0),
        name="unrope",
    )(dq, dkv, cos, sin)


def swap(value, axis, by=1):
    return lax.ppermute(value, axis, [(i, i ^ by) for i in range(lax.axis_size(axis))])


def onward(value):
    size = lax.axis_size("z")
    return lax.ppermute(value, "z", [(i, (i + 1) % size) for i in range(size)])


def low(value):
    return value.astype(LOW)


def wide(value):
    return value.astype(F32)


def plane_gather(value):
    if lax.axis_size("x") == 2:
        half = value.shape[0] // 2
        from_x, from_y = swap(value, "x"), swap(value, "y")
        top, bottom = swap(from_x[:half], "y"), swap(from_y[half:], "x")
        return [[value], [from_x], [from_y], [top, bottom]]
    row = [value] + [swap(value, "x", d) for d in range(1, lax.axis_size("x"))]
    return [[v] for v in row + [swap(v, "y") for v in row]]


def plane_scatter(parts):
    size = lax.axis_size("x")
    if size == 2:
        half = parts[0].shape[0] // 2
        top, bottom = swap(low(parts[3][:half]), "x"), swap(low(parts[3][half:]), "y")
        to_y = jnp.concatenate([low(wide(parts[2][:half]) + wide(top)), low(parts[2][half:])], 0)
        to_x = jnp.concatenate([low(parts[1][:half]), low(wide(parts[1][half:]) + wide(bottom))], 0)
        return wide(parts[0]) + wide(swap(to_x, "x")) + wide(swap(to_y, "y"))
    kept = [wide(parts[d]) + wide(swap(low(parts[size + d]), "y")) for d in range(size)]
    return sum([wide(swap(low(kept[d]), "x", d)) for d in range(1, size)], kept[0])


def ring_gather(value):
    chunks = [value]
    for _ in range(lax.axis_size("z") - 1):
        chunks.append(onward(chunks[-1]))
    return chunks


def ring_scatter(part_of, kind=LOW):
    size = lax.axis_size("z")
    total = part_of(1)
    for s in list(range(2, size)) + [0]:
        total = wide(part_of(s)) + wide(onward(total.astype(kind)))
    return total


def across(value):
    core = lax.axis_index("c")
    mine = lax.dynamic_index_in_dim(value, core, 0, keepdims=False)
    return jnp.concatenate([mine, swap(lax.dynamic_index_in_dim(value, 1 - core, 0, keepdims=False), "c")], 0)


def back_across(rows):
    core = lax.axis_index("c")
    tokens = rows.shape[0] // 2
    mine, other = rows[:tokens], wide(swap(low(rows[tokens:]), "c"))
    return jnp.stack([jnp.where(core == 0, mine, other), jnp.where(core == 0, other, mine)], 0)


def xor_blocks(value, blk, blocks):
    rows, width = value.shape[:-1], value.shape[-1]
    step = blocks // 2
    bit = 1
    while step >= 1:
        view = value.reshape(rows + (blocks // (2 * step), 2, width * step // blocks))
        flipped = jnp.concatenate([view[..., 1:, :], view[..., :1, :]], -2)
        value = jnp.where((blk // step) % 2 == 1, flipped, view).reshape(rows + (width,))
        step //= 2
    return value


def rms_unit(values):
    inverse = lax.rsqrt(jnp.mean(values * values, axis=-1, keepdims=True) + EPS)
    return values * inverse, inverse


def unit_backward(grad_unit, unit, inverse):
    return inverse * (grad_unit - unit * jnp.mean(grad_unit * unit, axis=-1, keepdims=True))


def place(chunks, rows_of, lead, tail):
    size = lax.axis_size("z")
    core, pos = lax.axis_index("c"), lax.axis_index("z")
    out = jnp.zeros(lead + (2, size) + tail, LOW)
    zeros = (0,) * len(tail)
    for dc in range(2):
        for s in range(size):
            start = (0,) * len(lead) + (core ^ dc, (pos - s) % size) + zeros
            out = lax.dynamic_update_slice(out, chunks[dc][s].reshape(lead + (1, 1) + tail), start)
    return out


def on_device(hidden_in, span_order, attn_gain, w_query, w_key, w_value, w_out, ffn_gain, w_gate, w_up, w_down, cotangent):
    seqs, tok, width = hidden_in.shape
    xs, zs = lax.axis_size("x"), lax.axis_size("z")
    chips = 2 * xs
    yi, xi, core, pos = lax.axis_index("y"), lax.axis_index("x"), lax.axis_index("c"), lax.axis_index("z")
    chip = yi * xs + xi
    blk = chip * 2 + core
    blocks = 2 * chips
    rows = w_query.shape[1]
    heads = HEADS // chips
    q_width = heads * HD
    all_width = q_width + 2 * HD

    per_span = zs // 2
    index = jnp.arange(zs * blocks, dtype=jnp.int32)
    its_blk = (chip ^ (index % blocks // 2)) * 2 + (core ^ (index % 2))
    its_pos = (pos - index // blocks) % zs
    its_span = 2 * its_blk + its_pos // per_span
    spans = jnp.arange(span_order.shape[0], dtype=jnp.int32)
    its_order = jnp.sum(jnp.where(its_span[:, None] == spans[None, :], span_order[None, :], 0), axis=1)
    places = its_order * per_span + its_pos % per_span
    order = jnp.sum(jnp.where(places[None, :] == index[:, None], index[None, :], 0), axis=1)
    query_places = places[:blocks]
    token_pos = (query_places[:, None] * tok + jnp.arange(tok, dtype=jnp.int32)[None, :]).reshape(-1)
    lane = jnp.arange(128, dtype=jnp.int32)
    inverse = 1.0 / THETA ** ((lane % (HD // 2)).astype(F32) * (2.0 / HD))
    angles = token_pos.astype(F32)[:, None] * inverse[None, :]
    cos = jnp.cos(angles)
    sin = jnp.sin(angles) * jnp.where(lane % HD < HD // 2, -1.0, 1.0)[None, :]

    gain_one = wide(attn_gain[0])[:, None]
    kv_of = [g * KV_HEADS // chips for g in range(chips)]
    own_cat = jnp.stack(
        [
            jnp.concatenate(
                [
                    w_query[0, :, g * q_width : (g + 1) * q_width],
                    w_key[0, :, kv_of[g] * HD : (kv_of[g] + 1) * HD],
                    w_value[0, :, kv_of[g] * HD : (kv_of[g] + 1) * HD],
                ],
                1,
            )
            for g in range(chips)
        ],
        0,
    )
    own_cat = low(wide(own_cat) * gain_one[None])

    def exchange(by_chip):
        got = jnp.zeros_like(by_chip)
        for d in range(chips):
            piece = lax.dynamic_index_in_dim(by_chip, chip ^ d, 0, keepdims=True)
            if d % xs:
                piece = swap(piece, "x", d % xs) if d < xs else lax.ppermute(
                    piece, ("y", "x"), [(i, i ^ d) for i in range(chips)]
                )
            elif d:
                piece = swap(piece, "y")
            got = lax.dynamic_update_slice(got, piece, (chip ^ d, 0, 0))
        return got

    by_ring = ring_gather(exchange(own_cat))
    qkv_w = place([by_ring, [swap(v, "c") for v in by_ring]], rows, (chips,), (rows, all_width)).reshape(width, all_width)

    unit_one, inverse_one = rms_unit(hidden_in)
    rows_one = jnp.concatenate(sum(plane_gather(across(low(unit_one))), []), 0)
    projected = jnp.dot(rows_one, qkv_w, preferred_element_type=F32)
    query, kv = rope(projected, cos, sin)
    kv_all = jnp.concatenate([v.reshape(blocks, tok, 2 * HD) for v in ring_gather(kv)], 0)
    attended, log_total = attn_fwd(order, query_places, query, kv_all)

    out_ring = ring_gather(w_out[0])
    out_w = place([out_ring, [swap(v, "c") for v in out_ring]], rows, (), (rows, width)).reshape(q_width, width)
    mixed = jnp.dot(attended, out_w, preferred_element_type=F32)
    chunk = 2 * tok
    middle = hidden_in + back_across(plane_scatter([mixed[d * chunk : (d + 1) * chunk] for d in range(chips)]))

    gain_ring = ring_gather(ffn_gain[0])
    gain_two = jnp.zeros((zs, rows), LOW)
    for s in range(zs):
        gain_two = lax.dynamic_update_slice(gain_two, gain_ring[s][None], ((pos - s) % zs, 0))
    gain_two = wide(gain_two.reshape(zs * rows, 1))

    def ffn_gather(shard):
        pieces = sum(plane_gather(shard), [])
        return jnp.concatenate(pieces + [swap(v, "c") for v in pieces], 0)

    gate_w = ffn_gather(low(wide(w_gate[0]) * gain_two))
    up_w = ffn_gather(low(wide(w_up[0]) * gain_two))
    down_w = ffn_gather(jnp.transpose(w_down[0]))

    rel = core * chips + chip

    def spread(value):
        both = value.reshape(seqs, tok, chips, 2, width // blocks)
        both = jnp.swapaxes(both, 2, 3).reshape(seqs, tok, width)
        both = xor_blocks(both, rel, blocks)
        first, second = ring_gather(both[0]), ring_gather(both[1])
        return jnp.concatenate(sum([[first[s], second[s]] for s in range(zs)], []), 0)

    def gathered_sum(parts):
        sums = jnp.stack([ring_scatter(lambda s, q=q: parts[s, q]) for q in range(seqs)], 0)
        both = xor_blocks(sums, rel, blocks).reshape(seqs, tok, 2, chips, width // blocks)
        return jnp.swapaxes(both, 2, 3).reshape(seqs, tok, width)

    unit_two, inverse_two = rms_unit(middle)
    rows_two = spread(low(unit_two))
    gate = jnp.dot(rows_two, gate_w, preferred_element_type=F32)
    up = jnp.dot(rows_two, up_w, preferred_element_type=F32)
    activated = low(jax.nn.silu(gate) * up)
    partial_out = low(jnp.einsum("rf,df->rd", activated, down_w, preferred_element_type=F32))
    hidden_out = middle + gathered_sum(partial_out.reshape(zs, seqs, tok, width))

    grad_rows = spread(low(cotangent))
    grad_act = jnp.dot(grad_rows, down_w, preferred_element_type=F32)
    sig = jax.nn.sigmoid(gate)
    grad_gate = low(grad_act * up * sig * (1.0 + gate * (1.0 - sig)))
    grad_up = low(grad_act * gate * sig)
    normed_part = low(
        jnp.einsum("rf,df->rd", grad_gate, gate_w, preferred_element_type=F32)
        + jnp.einsum("rf,df->rd", grad_up, up_w, preferred_element_type=F32)
    )
    grad_unit_two = gathered_sum(normed_part.reshape(zs, seqs, tok, width))
    grad_middle = cotangent + unit_backward(grad_unit_two, unit_two, inverse_two)

    def weight_grad(rows_in, rows_f):
        half = width // 2
        sent = low(jnp.einsum("rd,rf->df", rows_in[:, half:], rows_f, preferred_element_type=F32))
        kept = jnp.einsum("rd,rf->df", rows_in[:, :half], rows_f, preferred_element_type=F32)
        both = low(kept + wide(swap(sent, "c")))
        size = half // chips
        return plane_scatter([both[d * size : (d + 1) * size] for d in range(chips)])

    gate_sum = weight_grad(rows_two, grad_gate)
    up_sum = weight_grad(rows_two, grad_up)
    grad_down = jnp.transpose(weight_grad(grad_rows, activated))
    gain_part = jnp.sum(gate_sum * wide(w_gate[0]) + up_sum * wide(w_up[0]), axis=1).reshape(zs, rows)
    grad_ffn_gain = ring_scatter(
        lambda s: lax.dynamic_index_in_dim(gain_part, (pos - s) % zs, 0, keepdims=False), F32
    )

    grad_mid_rows = jnp.concatenate(sum(plane_gather(across(low(grad_middle))), []), 0)
    grad_attended = low(jnp.einsum("rd,qd->rq", grad_mid_rows, out_w, preferred_element_type=F32))
    grad_query, grad_kv = attn_bwd(order, query_places, query, kv_all, attended, grad_attended, log_total)
    grad_kv = ring_scatter(lambda s: grad_kv[s * blocks : (s + 1) * blocks].reshape(blocks * tok, 2 * HD))
    grads = unrope(grad_query, grad_kv, cos, sin)

    def core_ring_sum(full, lead, tail):
        view = full.reshape(lead + (2, zs) + tail)
        axis = len(lead)
        other = lax.dynamic_index_in_dim(view, 1 - core, axis, keepdims=False)
        both = wide(lax.dynamic_index_in_dim(view, core, axis, keepdims=False)) + wide(swap(other, "c"))
        both = low(both)
        return ring_scatter(lambda s: lax.dynamic_index_in_dim(both, (pos - s) % zs, axis, keepdims=False))

    out_part = low(jnp.einsum("rq,rd->qd", attended, grad_mid_rows, preferred_element_type=F32))
    grad_out_w = core_ring_sum(out_part, (), (rows, width))

    unit_part = low(jnp.einsum("rq,dq->rd", grads, qkv_w, preferred_element_type=F32))
    grad_unit_one = back_across(plane_scatter([unit_part[d * chunk : (d + 1) * chunk] for d in range(chips)]))
    grad_in = grad_middle + unit_backward(grad_unit_one, unit_one, inverse_one)

    qkv_part = low(jnp.einsum("rd,rq->dq", rows_one, grads, preferred_element_type=F32))
    qkv_sum = wide(exchange(low(core_ring_sum(qkv_part, (chips,), (rows, all_width)))))
    query_sum = jnp.swapaxes(qkv_sum[:, :, :q_width], 0, 1).reshape(rows, HEADS * HD)
    share = chips // KV_HEADS

    def heads_of(start):
        part = qkv_sum[:, :, start : start + HD].reshape(KV_HEADS, share, rows, HD).sum(1)
        return jnp.swapaxes(part, 0, 1).reshape(rows, KV_HEADS * HD)

    key_sum, value_sum = heads_of(q_width), heads_of(q_width + HD)
    grad_attn_gain = (
        jnp.sum(query_sum * wide(w_query[0]), axis=1)
        + jnp.sum(key_sum * wide(w_key[0]), axis=1)
        + jnp.sum(value_sum * wide(w_value[0]), axis=1)
    )

    return (
        hidden_out,
        grad_in,
        grad_attn_gain[None],
        (query_sum * gain_one)[None],
        (key_sum * gain_one)[None],
        (value_sum * gain_one)[None],
        grad_out_w[None],
        grad_ffn_gain[None],
        (gate_sum * gain_two)[None],
        (up_sum * gain_two)[None],
        grad_down[None],
    )


def solution(mesh):
    n_blk, n_head = mesh.shape["blk"], mesh.shape["head"]
    fine = Mesh(mesh.devices.reshape(2, n_blk // 4, 2, n_head), ("y", "x", "c", "z"))
    blk = ("y", "x", "c")
    every = ("y", "x", "c", "z")
    tokens = P(None, every, None)
    vector = P(None, every)
    return jax.shard_map(
        on_device,
        mesh=fine,
        in_specs=(
            tokens, P(), vector, tokens, tokens, tokens, tokens, vector,
            P(None, blk, "z"), P(None, blk, "z"), P(None, "z", blk), tokens,
        ),
        out_specs=(
            tokens, tokens, vector, tokens, tokens, tokens, tokens, vector,
            P(None, blk, "z"), P(None, blk, "z"), P(None, "z", blk),
        ),
        check_vma=False,
    )
```
